512 devices in a mesh: row: 32 (over z, x_hi), col: 16 (over x_lo, y, core).
Axes of the slice: x: 4 (x_hi: 2, x_lo: 2; x = x_hi * 2 + x_lo), y: 4, z: 16, core: 2. Of those that a mesh axis runs over, the one named last changes fastest.
Arguments:
- a_blocks: float32 [32, 16, 8, 128, 128], P('row', 'col'), may hold values from -6 to 6
- a_coords: int32 [32, 16, 2, 8], P('row', 'col'), may hold values from 0 to 63, as said below
- b_blocks: float32 [32, 16, 32, 128, 128], P('row', 'col'), may hold values from -0.5 to 0.5
- b_coords: int32 [32, 16, 2, 32], P('row', 'col'), may hold values from 0 to 31, as said below
Outputs:
- product: float32 [8192, 32768], P('row', 'col')
The draws below stay inside these ranges and needn't reach their ends.
Inputs may be any that keep to these rules, and one draw needn't show every extreme that they name: `a_coords`: each tile lists 8 distinct block positions, exactly 4 of them in each of its 2 column pieces of 32 block columns, with distinct block columns inside one piece; entry 0 is a block row below 2, entry 1 a block column below 64. `b_coords`: each tile lists 32 distinct block positions; entry 0 is a block row below 32, entry 1 a block column below 16.
All inputs are finite; a program needn't handle non-finite values.
Results may differ from the reference program's by a relative error of at most 0.0003.
Values sent between devices are 32-bit elements; how exact they have to be, the bound alone decides.
A program may use at most 64 MiB of HBM per device.

```python
import jax
import jax.numpy as jnp
from jax import lax

BS = 128
KB = 32
RB = 2
CB = 16
STEPS = 2
GROWS = 32
GCOLS = 16
KPC = 2
NA = 8
NB = 32
MROWS = 8192
MCOLS = 32768


def draw_a_coords(key, part):
    keys = jax.random.split(jax.random.fold_in(key, 11), GROWS * GCOLS)
    per_piece = NA // KPC

    def one_tile(tile_key):
        first, second = jax.random.split(tile_key)
        piece_keys = jax.random.split(first, KPC)

        def one_piece(piece_key, piece):
            col_key, row_key = jax.random.split(piece_key)
            columns = jax.random.permutation(col_key, KB)[:per_piece]
            rows = jax.random.randint(row_key, (per_piece,), 0, RB)
            return jnp.stack([rows, columns + piece * KB])
        pieces = jax.vmap(one_piece)(piece_keys, jnp.arange(KPC, dtype=jnp.int32))
        joined = jnp.transpose(pieces, (1, 0, 2)).reshape(2, NA)
        order = jax.random.permutation(second, NA)
        return joined[:, order]
    return jax.vmap(one_tile)(keys).reshape(GROWS, GCOLS, 2, NA).astype(jnp.int32)


def draw_b_coords(key, part):
    a_pos_all = draw_a_coords(key, part)
    keys = jax.random.split(jax.random.fold_in(key, 23), GROWS * GCOLS)
    per_piece = NA // KPC

    def one_tile(tile_key):
        chosen = jax.random.permutation(tile_key, KB * CB)[:NB]
        return jnp.stack([chosen // CB, chosen % CB])
    base = jax.vmap(one_tile)(keys).reshape(GROWS, GCOLS, 2, NB).astype(jnp.int32)
    pick_key = jax.random.fold_in(key, 37)
    row_key, step_key, fill_key = jax.random.split(pick_key, 3)
    rows_pick = jax.random.randint(row_key, (GCOLS,), 0, GROWS).astype(jnp.int32)
    steps_pick = jax.random.randint(step_key, (GCOLS,), 0, STEPS).astype(jnp.int32)
    fill_keys = jax.random.split(fill_key, GCOLS)
    columns_all = jnp.arange(GCOLS, dtype=jnp.int32)

    def worst_tile(grid_col, piece_row, step, tile_key):
        user_row = ((piece_row - step) % GROWS).astype(jnp.int32)
        owner = (piece_row // KPC).astype(jnp.int32)
        piece = (piece_row % KPC).astype(jnp.int32)
        a_pos = a_pos_all[user_row, owner]
        outside = (a_pos[1] // KB != piece).astype(jnp.int32)
        score = outside * NA + jnp.arange(NA, dtype=jnp.int32)
        order = jnp.argsort(score, stable=True)
        kcols = (a_pos[1][order[:per_piece]] % KB).astype(jnp.int32)
        chosen = jax.random.permutation(tile_key, per_piece * CB)[:NB]
        return jnp.stack([kcols[chosen // CB], chosen % CB]).astype(jnp.int32)
    worst = jax.vmap(worst_tile)(columns_all, rows_pick, steps_pick, fill_keys)
    base = base.at[rows_pick, columns_all].set(worst)
    return base.astype(jnp.int32)


def level_of(own_key, dims, cuts, least, top_value):
    def one(axis_at, shards_of):
        draws = jax.random.uniform(jax.random.fold_in(jax.random.fold_in(own_key, 6), axis_at), (shards_of,), jnp.float32, least / len(cuts), top_value / len(cuts))
        return jnp.repeat(jnp.exp(draws), dims[axis_at] // shards_of).reshape((-1,) + (1,) * (len(dims) - axis_at - 1))

    loudness = one(*cuts[0])
    for cut in cuts[1:]:
        loudness = loudness * one(*cut)
    return loudness


def gaussian(stream_key, dims, spread, reach, cuts=(), kind=jnp.bfloat16):
    level = level_of(stream_key, dims, cuts, -0.22, 0.18) if cuts else 1.0
    entries = jax.random.normal(stream_key, dims, jnp.float32) * spread * level
    return jnp.minimum(jnp.maximum(entries, -reach), reach).astype(kind)


def setup_inputs(seed: int = 0) -> dict:
    splits = jax.random.split(jax.random.key(seed), 5)
    a_blocks = gaussian(splits[0], (GROWS, GCOLS, NA, BS, BS), 1.0, 6.0, ((0, 32), (1, 16)), jnp.float32)
    a_coords = draw_a_coords(jax.random.fold_in(splits[4], 71), 0)
    b_blocks = gaussian(splits[2], (GROWS, GCOLS, NB, BS, BS), BS ** -0.5, 0.5, ((0, 32), (1, 16)), jnp.float32)
    b_coords = draw_b_coords(jax.random.fold_in(splits[4], 71), 0)
    return dict(a_blocks=a_blocks, a_coords=a_coords, b_blocks=b_blocks, b_coords=b_coords)


def tile_product(a_blk, a_pos, b_blk, b_pos, piece):
    high = lax.Precision.HIGHEST
    in_piece = (a_pos[1] // KB) == piece
    kcol = a_pos[1] % KB
    match = ((kcol[:, None] == b_pos[0][None, :]) & in_piece[:, None]).astype(jnp.float32)
    rowsel = (a_pos[0][None, :] == jnp.arange(RB, dtype=jnp.int32)[:, None]).astype(jnp.float32)
    coef = rowsel[:, None, :] * jnp.transpose(match)[None, :, :]
    wide = jnp.einsum("rbm,mxy->rbxy", coef, a_blk, precision=high)
    prods = jnp.einsum("rbxy,byz->rbxz", wide, b_blk, precision=high)
    colsel = (b_pos[1][None, :] == jnp.arange(CB, dtype=jnp.int32)[:, None]).astype(jnp.float32)
    out = jnp.einsum("cb,rbxz->rxcz", colsel, prods, precision=high)
    return out.reshape(RB * BS, CB * BS)


def reference(a_blocks, a_coords, b_blocks, b_coords):
    def one_tile(flat):
        row_idx = (flat // GCOLS).astype(jnp.int32)
        col_idx = (flat % GCOLS).astype(jnp.int32)
        total = jnp.zeros((RB * BS, CB * BS), jnp.float32)
        for step in range(STEPS):
            piece_row = ((row_idx + step) % GROWS).astype(jnp.int32)
            owner = (piece_row // KPC).astype(jnp.int32)
            half = (piece_row % KPC).astype(jnp.int32)
            total = total + tile_product(a_blocks[row_idx, owner], a_coords[row_idx, owner],
                                         b_blocks[piece_row, col_idx], b_coords[piece_row, col_idx], half)
        return total

    tiles = lax.map(one_tile, jnp.arange(GROWS * GCOLS, dtype=jnp.int32))
    tiles = tiles.reshape(GROWS, GCOLS, RB * BS, CB * BS)
    return jnp.transpose(tiles, (0, 2, 1, 3)).reshape(MROWS, MCOLS)
```

```python
import functools

import jax
import jax.numpy as jnp
from jax import lax
from jax.experimental import pallas as pl
from jax.experimental.pallas import tpu as pltpu
from jax.sharding import PartitionSpec as P

BS = 128
KB = 32
RB = 2
CB = 16
STEPS = 2
PIECE = 4
NB = 32
YS = 4
MESH = pl.DeviceIdType.MESH
CHUNKS = (2, 2, 4, 4, 4, 4, 4, 4, 2, 1, 1)
STARTS = tuple(sum(CHUNKS[:k]) for k in range(len(CHUNKS)))
NCH = len(CHUNKS)
BESIDE = 5
HALF = STARTS[BESIDE]
STOPS_ODD = ((0, 1, 2), (3,), (4,), ())
STOPS_EVEN = ((5,), (6,), (7,), (8, 9, 10))
S1, S1C, S2, S2C, S3, S4, S4C, NS = 0, 3, 6, 7, 8, 11, 12, 13
R1, RC, R2, R3, R4, NR = 0, 1, 2, 3, 6, 7


def kernel(
    a_hbm, a_crd, a_pos, b_hbm, b_crd, out,
    a_full, a_got, a_gcrd, a_spos, b_own, b_got, b_mid, b_ocrd, b_gcrd, m_crd,
    tab_v, tab, prods, total,
    local_sem, b_send, b_recv, m_send, m_recv, a_send, a_recv, ready,
):
    row = lax.axis_index("row")
    col = lax.axis_index("col")
    rows = lax.axis_size("row")
    cols = lax.axis_size("col")
    per_col = rows // cols
    evens = lax.rem(row, per_col) == 0
    odds = jnp.logical_not(evens)
    beside = row + 1 - 2 * lax.rem(row, per_col)
    above2 = lax.rem(row + rows - 2, rows)
    below2 = lax.rem(row + 2, rows)
    x, y, core = col // 8, lax.rem(col, 8) // 2, lax.rem(col, 2)

    def at(xx, yy, cc):
        return (row, xx * 8 + yy * 2 + cc)

    y_peers = [at(x, lax.rem(y + d, YS), core) for d in range(1, YS)]
    x_peer = at(1 - x, y, core)
    core_peer = at(x, y, 1 - core)

    barrier = pltpu.get_barrier_semaphore()
    peers = [(beside, col), *y_peers, x_peer, core_peer]
    for peer in peers:
        pl.semaphore_signal(barrier, inc=1, device_id=peer, device_id_type=MESH)

    pl.semaphore_signal(barrier, inc=1, device_id=(above2, col), device_id_type=MESH)

    own_copy = pltpu.make_async_copy(b_hbm, b_own, local_sem.at[0])
    own_copy.start()
    crd_copy = pltpu.make_async_copy(b_crd, b_ocrd, local_sem.at[3])
    crd_copy.start()
    prods[0, NB] = jnp.zeros((BS, BS), jnp.float32)
    prods[1, NB] = jnp.zeros((BS, BS), jnp.float32)

    halves, owners = [], []
    for s in range(STEPS):
        piece_row = lax.rem(row + s, rows)
        owners.append(piece_row // per_col)
        halves.append(lax.rem(piece_row, per_col))

    def ranked(pos, half):
        places, count = [], 0
        for e in range(2 * PIECE):
            inside = pos(1, e) // KB == half
            places.append(jnp.where(inside, count, -1))
            count = count + inside.astype(jnp.int32)
        return places

    for s in range(STEPS):

        @pl.when(owners[s] == col)
        def _():
            load = pltpu.make_async_copy(a_hbm, a_full, local_sem.at[1])
            load.start()
            crd = pltpu.make_async_copy(a_crd, a_gcrd.at[s], local_sem.at[2])
            crd.start()
            load.wait()
            crd.wait()
            places = ranked(lambda i, e: a_pos[i, e], halves[s])
            for m in range(PIECE):
                which = 0
                for e in range(2 * PIECE):
                    which = which + jnp.where(places[e] == m, e, 0)
                a_got[s, m] = a_full[which]

    pl.semaphore_wait(barrier, len(peers) + 1)
    pl.semaphore_signal(ready, inc=1, device_id=(below2, col), device_id_type=MESH)

    def remote(src, dst, send, recv, device):
        return pltpu.make_async_remote_copy(
            src_ref=src, dst_ref=dst, send_sem=send, recv_sem=recv,
            device_id=device, device_id_type=MESH,
        )

    crd_direct = remote(b_crd, b_gcrd, b_send.at[NCH], b_recv.at[NCH], (beside, col))
    crd_first = remote(b_crd, m_crd, b_send.at[NCH], m_recv.at[NCH], (beside, col))
    crd_second = remote(m_crd, b_gcrd, m_send.at[NCH], b_recv.at[NCH], (above2, col))
    direct, first, second = [], [], []
    for k in range(NCH):
        part = pl.ds(STARTS[k], CHUNKS[k])
        mid = b_mid.at[pl.ds(STARTS[k] % HALF, CHUNKS[k])]
        hops = (beside, above2) if k < BESIDE else (above2, beside)
        direct.append(
            remote(b_hbm.at[part], b_got.at[part], b_send.at[k], b_recv.at[k], (beside, col))
        )
        first.append(remote(b_hbm.at[part], mid, b_send.at[k], m_recv.at[k], (hops[0], col)))
        second.append(remote(mid, b_got.at[part], m_send.at[k], b_recv.at[k], (hops[1], col)))

    def stop(i):
        @pl.when(odds)
        def _():
            if i == 0:
                pl.semaphore_wait(ready, 1)
                crd_first.wait_recv()
                crd_second.start()
            for k in STOPS_ODD[i]:
                first[k].wait_recv()
                second[k].start()

        @pl.when(evens)
        def _():
            for k in STOPS_EVEN[i]:
                first[k].wait_recv()
                second[k].start()

    def step_copies(s):
        blocks, crd = a_got.at[s], a_gcrd.at[s]
        send, recv = a_send.at[s], a_recv.at[s]
        theirs = [blocks.at[pl.ds(lax.rem(y + d, YS), 1)] for d in range(1, YS)]
        mine = blocks.at[pl.ds(y, 1)]
        one = [remote(theirs[d], theirs[d], send.at[S1 + d], recv.at[R1], y_peers[d]) for d in range(3)]
        one_crd = [remote(crd, crd, send.at[S1C + d], recv.at[RC], y_peers[d]) for d in range(3)]
        two = remote(mine, mine, send.at[S2], recv.at[R2], x_peer)
        two_crd = remote(crd, crd, send.at[S2C], recv.at[RC], x_peer)
        three = [remote(mine, mine, send.at[S3 + d], recv.at[R3 + d], y_peers[d]) for d in range(3)]
        four = remote(blocks, blocks, send.at[S4], recv.at[R4], core_peer)
        four_crd = remote(crd, crd, send.at[S4C], recv.at[RC], core_peer)
        return one, one_crd, two, two_crd, three, four, four_crd

    own_x = [owner // 8 for owner in owners]
    own_y = [lax.rem(owner, 8) // 2 for owner in owners]
    own_core = [lax.rem(owner, 2) for owner in owners]
    is_owner = [owner == col for owner in owners]
    holds = [(own_core[s] == core) & (own_x[s] == x) for s in range(STEPS)]

    def not_owner(s, d):
        return (own_x[s] != x) | (own_y[s] != lax.rem(y + 1 + d, YS))

    for s in range(STEPS):
        one, one_crd, two, two_crd, *_ = step_copies(s)

        @pl.when(is_owner[s])
        def _():
            for copy in [two_crd, two] + one_crd + one:
                copy.start()

    @pl.when(evens)
    def _():
        crd_first.start()
        first[0].start()

    @pl.when(odds)
    def _():
        crd_direct.start()
        direct[0].start()

    for s in range(STEPS):
        one, one_crd, two, two_crd, *_ = step_copies(s)

        @pl.when(holds[s] & jnp.logical_not(is_owner[s]))
        def _():
            one_crd[0].wait_recv()
            one[0].wait_recv()
            two_crd.start()
            two.start()

    @pl.when(odds)
    def _():
        for copy in direct[1:]:
            copy.start()

    @pl.when(evens)
    def _():
        for copy in first[1:BESIDE]:
            copy.start()
        pl.semaphore_wait(ready, 1)
        for copy in first[BESIDE:]:
            copy.start()

    for s in range(STEPS):
        one, one_crd, two, two_crd, three, four, four_crd = step_copies(s)

        @pl.when(own_core[s] == core)
        def _():
            @pl.when(own_x[s] != x)
            def _():
                two_crd.wait_recv()
                two.wait_recv()

            for d in range(3):
                pl.when(not_owner(s, d))(three[d].start)

            @pl.when(jnp.logical_not(is_owner[s]))
            def _():
                for copy in three:
                    copy.wait_recv()

            four_crd.start()
            four.start()

        @pl.when(own_core[s] != core)
        def _():
            four_crd.wait_recv()
            four.wait_recv()

        to_smem = pltpu.make_async_copy(a_gcrd.at[s], a_spos.at[s], local_sem.at[2])
        to_smem.start()
        to_smem.wait()

    stop(0)
    crd_direct.wait_recv()
    crd_copy.wait()

    picks = []
    for s in range(STEPS):
        places = ranked(lambda i, e: a_spos[s, i, e], halves[s])
        k_of, r_of = [], []
        for m in range(PIECE):
            k_m, r_m = 0, 0
            for e in range(2 * PIECE):
                k_m = k_m + jnp.where(places[e] == m, a_spos[s, 1, e], 0)
                r_m = r_m + jnp.where(places[e] == m, a_spos[s, 0, e], 0)
            k_of.append(k_m - halves[s] * KB)
            r_of.append(r_m)
        crd = b_ocrd if s == 0 else b_gcrd
        key = jnp.full((1, NB), PIECE * CB, jnp.int32)
        for m in range(PIECE):
            key = jnp.where(crd[0:1, :] == k_of[m], m * CB + crd[1:2, :], key)
        slot = lax.broadcasted_iota(jnp.int32, (PIECE * CB, NB), 0)
        entry = lax.broadcasted_iota(jnp.int32, (PIECE * CB, NB), 1)
        found = jnp.min(jnp.where(key == slot, entry, NB), axis=1, keepdims=True)
        tab_v[s, pl.ds(0, PIECE * CB), :] = jnp.broadcast_to(found, (PIECE * CB, BS))
        tab_v[s, pl.ds(PIECE * CB, 1), pl.ds(0, NB)] = jnp.minimum(key // CB, PIECE - 1)
        to_smem = pltpu.make_async_copy(tab_v.at[s], tab.at[s], local_sem.at[2])
        to_smem.start()
        to_smem.wait()
        picks.append(r_of)

    def multiply(s, blocks, first, count):
        def one_block(i, carry):
            n = first + i
            m = tab[s, PIECE * CB, n]
            prods[s, n] = jnp.dot(
                a_got[s, m], blocks[n],
                precision=lax.Precision.HIGHEST, preferred_element_type=jnp.float32,
            )
            return carry

        lax.fori_loop(0, count, one_block, 0, unroll=min(4, count))

    def gathered(s, c, r):
        terms = []
        for m in range(PIECE):
            n = jnp.where(picks[s][m] == r, tab[s, m * CB + c, 0], NB)
            terms.append(prods[s, n])
        return (terms[0] + terms[1]) + (terms[2] + terms[3])

    stop(1)
    own_copy.wait()
    multiply(0, b_own, 0, NB)
    stop(2)

    def first_term(c, carry):
        for r in range(RB):
            total[pl.ds(r * BS, BS), pl.ds(pl.multiple_of(c * BS, BS), BS)] = gathered(0, c, r)
        return carry

    lax.fori_loop(0, CB, first_term, 0, unroll=4)

    stop(3)
    for k in range(NCH):
        direct[k].wait_recv()
        multiply(1, b_got, STARTS[k], CHUNKS[k])

    def second_term(c, carry):
        for r in range(RB):
            spot = (pl.ds(r * BS, BS), pl.ds(pl.multiple_of(c * BS, BS), BS))
            out[spot] = total[spot] + gathered(1, c, r)
        return carry

    lax.fori_loop(0, CB, second_term, 0, unroll=4)

    for s in range(STEPS):
        one, one_crd, two, two_crd, three, four, four_crd = step_copies(s)

        @pl.when(is_owner[s])
        def _():
            for copy in one_crd + one:
                copy.wait_send()

        @pl.when(holds[s])
        def _():
            two_crd.wait_send()
            two.wait_send()

        @pl.when(own_core[s] == core)
        def _():
            for d in range(3):
                pl.when(not_owner(s, d))(three[d].wait_send)
            four_crd.wait_send()
            four.wait_send()

    crd_direct.wait_send()
    for copy in direct:
        copy.wait_send()

    @pl.when(evens)
    def _():
        for copy in second[BESIDE:]:
            copy.wait_send()

    @pl.when(odds)
    def _():
        for copy in [crd_second] + second[:BESIDE]:
            copy.wait_send()


def per_device(a_blocks, a_coords, b_blocks, b_coords):
    hbm = pl.BlockSpec(memory_space=pltpu.HBM)
    smem = pl.BlockSpec(memory_space=pltpu.SMEM)
    a_blk, a_pos = a_blocks[0, 0], a_coords[0, 0]
    b_blk, b_pos = b_blocks[0, 0], b_coords[0, 0]
    f32, i32 = jnp.float32, jnp.int32

    def kept(value):
        return pltpu.with_memory_space_constraint(value, pltpu.HBM)

    return pl.pallas_call(
        kernel,
        out_shape=jax.ShapeDtypeStruct((RB * BS, CB * BS), f32),
        in_specs=[hbm, hbm, smem, hbm, hbm],
        out_specs=pl.BlockSpec(memory_space=pltpu.VMEM),
        scratch_shapes=[
            pltpu.VMEM((2 * PIECE, BS, BS), f32),
            pltpu.VMEM((STEPS, PIECE, BS, BS), f32),
            pltpu.VMEM((STEPS, 2, 2 * PIECE), i32),
            pltpu.SMEM((STEPS, 2, 2 * PIECE), i32),
            pltpu.VMEM((NB, BS, BS), f32),
            pltpu.VMEM((NB, BS, BS), f32),
            pltpu.VMEM((HALF, BS, BS), f32),
            pltpu.VMEM((2, NB), i32),
            pltpu.VMEM((2, NB), i32),
            pltpu.VMEM((2, NB), i32),
            pltpu.VMEM((STEPS, PIECE * CB + 8, BS), i32),
            pltpu.SMEM((STEPS, PIECE * CB + 8, BS), i32),
            pltpu.VMEM((STEPS, NB + 1, BS, BS), f32),
            pltpu.VMEM((RB * BS, CB * BS), f32),
            pltpu.SemaphoreType.DMA((4,)),
            pltpu.SemaphoreType.DMA((NCH + 1,)),
            pltpu.SemaphoreType.DMA((NCH + 1,)),
            pltpu.SemaphoreType.DMA((NCH + 1,)),
            pltpu.SemaphoreType.DMA((NCH + 1,)),
            pltpu.SemaphoreType.DMA((STEPS, NS)),
            pltpu.SemaphoreType.DMA((STEPS, NR)),
            pltpu.SemaphoreType.REGULAR,
        ],
        compiler_params=pltpu.CompilerParams(
            collective_id=0, has_side_effects=True, vmem_limit_bytes=48 << 20
        ),
    )(kept(a_blk), kept(a_pos), a_pos, kept(b_blk), kept(b_pos))


def solution(mesh):
    return jax.shard_map(
        per_device,
        mesh=mesh,
        in_specs=(
            P("row", "col", None, None, None),
            P("row", "col", None, None),
            P("row", "col", None, None, None),
            P("row", "col", None, None),
        ),
        out_specs=P("row", "col"),
        check_vma=False,
    )
```

```python
import functools

import jax
import jax.numpy as jnp
from jax import lax
from jax.experimental import pallas as pl
from jax.experimental.pallas import tpu as pltpu
from jax.sharding import PartitionSpec as P

BS = 128
KB = 32
RB = 2
CB = 16
STEPS = 2
PIECE = 4
NB = 32
YS = 4
MESH = pl.DeviceIdType.MESH
CHUNKS = (4, 2, 2, 4, 4, 4, 4, 4, 2, 1, 1)
STARTS = tuple(sum(CHUNKS[:k]) for k in range(len(CHUNKS)))
NCH = len(CHUNKS)
BESIDE = 5
HALF = STARTS[BESIDE]
STOPS_ODD = ((0,), (1, 2), (3,), (4,), ())
STOPS_EVEN = ((), (5,), (6,), (7,), (8, 9, 10))
S1, S1C, S2, S2C, S3, S4, S4C, NS = 0, 3, 6, 7, 8, 11, 12, 13
R1, RC, R2, R3, R4, NR = 0, 1, 2, 3, 6, 7


def kernel(
    a_hbm, a_crd, a_pos, b_hbm, b_crd, out,
    a_full, a_got, a_gcrd, a_spos, b_own, b_got, b_mid, b_ocrd, b_gcrd, m_crd,
    tab_v, tab, prods, total,
    local_sem, b_send, b_recv, m_send, m_recv, a_send, a_recv, ready,
):
    row = lax.axis_index("row")
    col = lax.axis_index("col")
    rows = lax.axis_size("row")
    cols = lax.axis_size("col")
    per_col = rows // cols
    evens = lax.rem(row, per_col) == 0
    odds = jnp.logical_not(evens)
    beside = row + 1 - 2 * lax.rem(row, per_col)
    above2 = lax.rem(row + rows - 2, rows)
    below2 = lax.rem(row + 2, rows)
    x, y, core = col // 8, lax.rem(col, 8) // 2, lax.rem(col, 2)

    def at(xx, yy, cc):
        return (row, xx * 8 + yy * 2 + cc)

    y_peers = [at(x, lax.rem(y + d, YS), core) for d in range(1, YS)]
    x_peer = at(1 - x, y, core)
    core_peer = at(x, y, 1 - core)

    halves, owners = [], []
    for s in range(STEPS):
        piece_row = lax.rem(row + s, rows)
        owners.append(piece_row // per_col)
        halves.append(lax.rem(piece_row, per_col))

    own_x = [owner // 8 for owner in owners]
    own_y = [lax.rem(owner, 8) // 2 for owner in owners]
    own_core = [lax.rem(owner, 2) for owner in owners]
    is_owner = [owner == col for owner in owners]
    holds = [(own_core[s] == core) & (own_x[s] == x) for s in range(STEPS)]

    in_line = (own_core[0] == core) | (own_core[1] == core)
    off_line = (own_core[0] != core) | (own_core[1] != core)
    sends_x = holds[0] | holds[1]
    gets_x = ((own_core[0] == core) & (own_x[0] != x)) | ((own_core[1] == core) & (own_x[1] != x))

    barrier = pltpu.get_barrier_semaphore()

    def greet(peer):
        pl.semaphore_signal(barrier, inc=1, device_id=peer, device_id_type=MESH)

    greet((beside, col))
    greet((above2, col))

    @pl.when(in_line)
    def _():
        for peer in y_peers:
            greet(peer)

    pl.when(gets_x)(lambda: greet(x_peer))
    pl.when(off_line)(lambda: greet(core_peer))
    greeted = 2 + (YS - 1 + 1) * in_line.astype(jnp.int32) + sends_x.astype(jnp.int32)

    own_copy = pltpu.make_async_copy(b_hbm, b_own, local_sem.at[0])
    own_copy.start()
    crd_copy = pltpu.make_async_copy(b_crd, b_ocrd, local_sem.at[3])
    crd_copy.start()
    prods[0, NB] = jnp.zeros((BS, BS), jnp.float32)
    prods[1, NB] = jnp.zeros((BS, BS), jnp.float32)

    def ranked(pos, half):
        places, count = [], 0
        for e in range(2 * PIECE):
            inside = pos(1, e) // KB == half
            places.append(jnp.where(inside, count, -1))
            count = count + inside.astype(jnp.int32)
        return places

    for s in range(STEPS):

        @pl.when(owners[s] == col)
        def _():
            load = pltpu.make_async_copy(a_hbm, a_full, local_sem.at[1])
            load.start()
            crd = pltpu.make_async_copy(a_crd, a_gcrd.at[s], local_sem.at[2])
            crd.start()
            load.wait()
            crd.wait()
            places = ranked(lambda i, e: a_pos[i, e], halves[s])
            for m in range(PIECE):
                which = 0
                for e in range(2 * PIECE):
                    which = which + jnp.where(places[e] == m, e, 0)
                a_got[s, m] = a_full[which]

    pl.semaphore_wait(barrier, greeted)
    pl.semaphore_signal(ready, inc=1, device_id=(below2, col), device_id_type=MESH)

    def remote(src, dst, send, recv, device):
        return pltpu.make_async_remote_copy(
            src_ref=src, dst_ref=dst, send_sem=send, recv_sem=recv,
            device_id=device, device_id_type=MESH,
        )

    crd_direct = remote(b_crd, b_gcrd, b_send.at[NCH], b_recv.at[NCH], (beside, col))
    crd_first = remote(b_crd, m_crd, b_send.at[NCH], m_recv.at[NCH], (beside, col))
    crd_second = remote(m_crd, b_gcrd, m_send.at[NCH], b_recv.at[NCH], (above2, col))
    direct, first, second = [], [], []
    for k in range(NCH):
        part = pl.ds(STARTS[k], CHUNKS[k])
        mid = b_mid.at[pl.ds(STARTS[k] % HALF, CHUNKS[k])]
        hops = (beside, above2) if k < BESIDE else (above2, beside)
        direct.append(
            remote(b_hbm.at[part], b_got.at[part], b_send.at[k], b_recv.at[k], (beside, col))
        )
        first.append(remote(b_hbm.at[part], mid, b_send.at[k], m_recv.at[k], (hops[0], col)))
        second.append(remote(mid, b_got.at[part], m_send.at[k], b_recv.at[k], (hops[1], col)))

    def stop(i):
        @pl.when(odds)
        def _():
            if i == 0:
                pl.semaphore_wait(ready, 1)
                crd_first.wait_recv()
                crd_second.start()
            for k in STOPS_ODD[i]:
                first[k].wait_recv()
                second[k].start()

        @pl.when(evens)
        def _():
            for k in STOPS_EVEN[i]:
                first[k].wait_recv()
                second[k].start()

    def step_copies(s):
        blocks, crd = a_got.at[s], a_gcrd.at[s]
        send, recv = a_send.at[s], a_recv.at[s]
        theirs = [blocks.at[pl.ds(lax.rem(y + d, YS), 1)] for d in range(1, YS)]
        mine = blocks.at[pl.ds(y, 1)]
        one = [remote(theirs[d], theirs[d], send.at[S1 + d], recv.at[R1], y_peers[d]) for d in range(3)]
        one_crd = [remote(crd, crd, send.at[S1C + d], recv.at[RC], y_peers[d]) for d in range(3)]
        two = remote(mine, mine, send.at[S2], recv.at[R2], x_peer)
        two_crd = remote(crd, crd, send.at[S2C], recv.at[RC], x_peer)
        three = [remote(mine, mine, send.at[S3 + d], recv.at[R3 + d], y_peers[d]) for d in range(3)]
        four = remote(blocks, blocks, send.at[S4], recv.at[R4], core_peer)
        four_crd = remote(crd, crd, send.at[S4C], recv.at[RC], core_peer)
        return one, one_crd, two, two_crd, three, four, four_crd

    def not_owner(s, d):
        return (own_x[s] != x) | (own_y[s] != lax.rem(y + 1 + d, YS))

    for s in range(STEPS):
        one, one_crd, two, two_crd, *_ = step_copies(s)

        @pl.when(is_owner[s])
        def _():
            for copy in [two_crd, two] + one_crd + one:
                copy.start()

    @pl.when(evens)
    def _():
        crd_first.start()
        first[0].start()

    @pl.when(odds)
    def _():
        crd_direct.start()
        direct[0].start()

    for s in range(STEPS):
        one, one_crd, two, two_crd, *_ = step_copies(s)

        @pl.when(holds[s] & jnp.logical_not(is_owner[s]))
        def _():
            one_crd[0].wait_recv()
            one[0].wait_recv()
            two_crd.start()
            two.start()

    @pl.when(odds)
    def _():
        for copy in direct[1:]:
            copy.start()

    @pl.when(evens)
    def _():
        for copy in first[1:BESIDE]:
            copy.start()
        pl.semaphore_wait(ready, 1)
        for copy in first[BESIDE:]:
            copy.start()

    for s in range(STEPS):
        stop(s)
        one, one_crd, two, two_crd, three, four, four_crd = step_copies(s)

        @pl.when(own_core[s] == core)
        def _():
            @pl.when(own_x[s] != x)
            def _():
                two_crd.wait_recv()
                two.wait_recv()

            for d in range(3):
                pl.when(not_owner(s, d))(three[d].start)

            @pl.when(jnp.logical_not(is_owner[s]))
            def _():
                for copy in three:
                    copy.wait_recv()

            four_crd.start()
            four.start()

        @pl.when(own_core[s] != core)
        def _():
            four_crd.wait_recv()
            four.wait_recv()

        to_smem = pltpu.make_async_copy(a_gcrd.at[s], a_spos.at[s], local_sem.at[2])
        to_smem.start()
        to_smem.wait()

    stop(2)
    crd_direct.wait_recv()
    crd_copy.wait()

    picks = []
    for s in range(STEPS):
        places = ranked(lambda i, e: a_spos[s, i, e], halves[s])
        k_of, r_of = [], []
        for m in range(PIECE):
            k_m, r_m = 0, 0
            for e in range(2 * PIECE):
                k_m = k_m + jnp.where(places[e] == m, a_spos[s, 1, e], 0)
                r_m = r_m + jnp.where(places[e] == m, a_spos[s, 0, e], 0)
            k_of.append(k_m - halves[s] * KB)
            r_of.append(r_m)
        crd = b_ocrd if s == 0 else b_gcrd
        key = jnp.full((1, NB), PIECE * CB, jnp.int32)
        for m in range(PIECE):
            key = jnp.where(crd[0:1, :] == k_of[m], m * CB + crd[1:2, :], key)
        slot = lax.broadcasted_iota(jnp.int32, (PIECE * CB, NB), 0)
        entry = lax.broadcasted_iota(jnp.int32, (PIECE * CB, NB), 1)
        found = jnp.min(jnp.where(key == slot, entry, NB), axis=1, keepdims=True)
        tab_v[s, pl.ds(0, PIECE * CB), :] = jnp.broadcast_to(found, (PIECE * CB, BS))
        tab_v[s, pl.ds(PIECE * CB, 1), pl.ds(0, NB)] = jnp.minimum(key // CB, PIECE - 1)
        to_smem = pltpu.make_async_copy(tab_v.at[s], tab.at[s], local_sem.at[2])
        to_smem.start()
        to_smem.wait()
        picks.append(r_of)

    def multiply(s, blocks, first, count):
        def one_block(i, carry):
            n = first + i
            m = tab[s, PIECE * CB, n]
            prods[s, n] = jnp.dot(
                a_got[s, m], blocks[n],
                precision=lax.Precision.HIGHEST, preferred_element_type=jnp.float32,
            )
            return carry

        lax.fori_loop(0, count, one_block, 0, unroll=min(4, count))

    def gathered(s, c, r):
        terms = []
        for m in range(PIECE):
            n = jnp.where(picks[s][m] == r, tab[s, m * CB + c, 0], NB)
            terms.append(prods[s, n])
        return (terms[0] + terms[1]) + (terms[2] + terms[3])

    own_copy.wait()
    multiply(0, b_own, 0, NB)
    stop(3)

    def first_term(c, carry):
        for r in range(RB):
            total[pl.ds(r * BS, BS), pl.ds(pl.multiple_of(c * BS, BS), BS)] = gathered(0, c, r)
        return carry

    lax.fori_loop(0, CB, first_term, 0, unroll=4)

    stop(4)
    for k in range(NCH):
        direct[k].wait_recv()
        multiply(1, b_got, STARTS[k], CHUNKS[k])

    def second_term(c, carry):
        for r in range(RB):
            spot = (pl.ds(r * BS, BS), pl.ds(pl.multiple_of(c * BS, BS), BS))
            out[spot] = total[spot] + gathered(1, c, r)
        return carry

    lax.fori_loop(0, CB, second_term, 0, unroll=4)

    for s in range(STEPS):
        one, one_crd, two, two_crd, three, four, four_crd = step_copies(s)

        @pl.when(is_owner[s])
        def _():
            for copy in one_crd + one:
                copy.wait_send()

        @pl.when(holds[s])
        def _():
            two_crd.wait_send()
            two.wait_send()

        @pl.when(own_core[s] == core)
        def _():
            for d in range(3):
                pl.when(not_owner(s, d))(three[d].wait_send)
            four_crd.wait_send()
            four.wait_send()

    crd_direct.wait_send()
    for copy in direct:
        copy.wait_send()

    @pl.when(evens)
    def _():
        for copy in second[BESIDE:]:
            copy.wait_send()

    @pl.when(odds)
    def _():
        for copy in [crd_second] + second[:BESIDE]:
            copy.wait_send()


def per_device(a_blocks, a_coords, b_blocks, b_coords):
    hbm = pl.BlockSpec(memory_space=pltpu.HBM)
    smem = pl.BlockSpec(memory_space=pltpu.SMEM)
    a_blk, a_pos = a_blocks[0, 0], a_coords[0, 0]
    b_blk, b_pos = b_blocks[0, 0], b_coords[0, 0]
    f32, i32 = jnp.float32, jnp.int32

    def kept(value):
        return pltpu.with_memory_space_constraint(value, pltpu.HBM)

    return pl.pallas_call(
        kernel,
        out_shape=jax.ShapeDtypeStruct((RB * BS, CB * BS), f32),
        in_specs=[hbm, hbm, smem, hbm, hbm],
        out_specs=pl.BlockSpec(memory_space=pltpu.VMEM),
        scratch_shapes=[
            pltpu.VMEM((2 * PIECE, BS, BS), f32),
            pltpu.VMEM((STEPS, PIECE, BS, BS), f32),
            pltpu.VMEM((STEPS, 2, 2 * PIECE), i32),
            pltpu.SMEM((STEPS, 2, 2 * PIECE), i32),
            pltpu.VMEM((NB, BS, BS), f32),
            pltpu.VMEM((NB, BS, BS), f32),
            pltpu.VMEM((HALF, BS, BS), f32),
            pltpu.VMEM((2, NB), i32),
            pltpu.VMEM((2, NB), i32),
            pltpu.VMEM((2, NB), i32),
            pltpu.VMEM((STEPS, PIECE * CB + 8, BS), i32),
            pltpu.SMEM((STEPS, PIECE * CB + 8, BS), i32),
            pltpu.VMEM((STEPS, NB + 1, BS, BS), f32),
            pltpu.VMEM((RB * BS, CB * BS), f32),
            pltpu.SemaphoreType.DMA((4,)),
            pltpu.SemaphoreType.DMA((NCH + 1,)),
            pltpu.SemaphoreType.DMA((NCH + 1,)),
            pltpu.SemaphoreType.DMA((NCH + 1,)),
            pltpu.SemaphoreType.DMA((NCH + 1,)),
            pltpu.SemaphoreType.DMA((STEPS, NS)),
            pltpu.SemaphoreType.DMA((STEPS, NR)),
            pltpu.SemaphoreType.REGULAR,
        ],
        compiler_params=pltpu.CompilerParams(
            collective_id=0, has_side_effects=True, vmem_limit_bytes=48 << 20
        ),
    )(kept(a_blk), kept(a_pos), a_pos, kept(b_blk), kept(b_pos))


def solution(mesh):
    return jax.shard_map(
        per_device,
        mesh=mesh,
        in_specs=(
            P("row", "col", None, None, None),
            P("row", "col", None, None),
            P("row", "col", None, None, None),
            P("row", "col", None, None),
        ),
        out_specs=P("row", "col"),
        check_vma=False,
    )
```

```python
import functools

import jax
import jax.numpy as jnp
from jax import lax
from jax.experimental import pallas as pl
from jax.experimental.pallas import tpu as pltpu
from jax.sharding import PartitionSpec as P

BS = 128
KB = 32
RB = 2
CB = 16
STEPS = 2
PIECE = 4
NB = 32
YS = 4
MESH = pl.DeviceIdType.MESH
CHUNKS = (6, 2, 4, 4, 4, 4, 4, 2, 1, 1)
STARTS = tuple(sum(CHUNKS[:k]) for k in range(len(CHUNKS)))
NCH = len(CHUNKS)
BESIDE = 4
HALF = STARTS[BESIDE]
LATE = 2
EARLY = STARTS[NCH - LATE]
STOPS_ODD = ((0,), (1,), (2,), (3,), ())
STOPS_EVEN = ((), (4,), (5,), (6,), (7, 8, 9))
S1, S1C, S2, S2C, S3, S4, S4C, NS = 0, 3, 6, 7, 8, 11, 12, 13
R1, RC, R2, R3, R4, NR = 0, 1, 2, 3, 6, 7


def kernel(
    a_hbm, a_crd, a_pos, b_hbm, b_crd, out,
    a_full, a_got, a_gcrd, a_spos, b_own, b_got, b_mid, b_ocrd, b_gcrd, m_crd,
    tab_v, tab, prods, total,
    local_sem, b_send, b_recv, m_send, m_recv, a_send, a_recv, ready, line_ready,
):
    row = lax.axis_index("row")
    col = lax.axis_index("col")
    rows = lax.axis_size("row")
    cols = lax.axis_size("col")
    per_col = rows // cols
    evens = lax.rem(row, per_col) == 0
    odds = jnp.logical_not(evens)
    beside = row + 1 - 2 * lax.rem(row, per_col)
    above2 = lax.rem(row + rows - 2, rows)
    below2 = lax.rem(row + 2, rows)
    x, y, core = col // 8, lax.rem(col, 8) // 2, lax.rem(col, 2)

    def at(xx, yy, cc):
        return (row, xx * 8 + yy * 2 + cc)

    y_peers = [at(x, lax.rem(y + d, YS), core) for d in range(1, YS)]
    x_peer = at(1 - x, y, core)
    core_peer = at(x, y, 1 - core)

    halves, owners = [], []
    for s in range(STEPS):
        piece_row = lax.rem(row + s, rows)
        owners.append(piece_row // per_col)
        halves.append(lax.rem(piece_row, per_col))

    own_x = [owner // 8 for owner in owners]
    own_y = [lax.rem(owner, 8) // 2 for owner in owners]
    own_core = [lax.rem(owner, 2) for owner in owners]
    is_owner = [owner == col for owner in owners]
    holds = [(own_core[s] == core) & (own_x[s] == x) for s in range(STEPS)]

    in_line = (own_core[0] == core) | (own_core[1] == core)
    off_line = (own_core[0] != core) | (own_core[1] != core)
    sends_x = holds[0] | holds[1]
    gets_x = ((own_core[0] == core) & (own_x[0] != x)) | ((own_core[1] == core) & (own_x[1] != x))

    barrier = pltpu.get_barrier_semaphore()

    def greet(peer):
        pl.semaphore_signal(barrier, inc=1, device_id=peer, device_id_type=MESH)

    greet((beside, col))
    first_plane = row < per_col
    last_plane = row >= rows - per_col

    pl.when(jnp.logical_not(last_plane))(lambda: greet((below2, col)))
    pl.when(first_plane)(lambda: greet((above2, col)))

    for d in range(1, YS):
        pl.when(in_line & (y + d < YS))(lambda: greet(y_peers[d - 1]))

    pl.when(gets_x)(lambda: greet(x_peer))
    pl.when(off_line)(lambda: greet(core_peer))
    greeted = 1 + jnp.logical_not(first_plane).astype(jnp.int32) + last_plane.astype(jnp.int32)
    greeted = greeted + (y + 1) * in_line.astype(jnp.int32) + sends_x.astype(jnp.int32)

    own_copy = pltpu.make_async_copy(b_hbm, b_own, local_sem.at[0])
    own_copy.start()
    crd_copy = pltpu.make_async_copy(b_crd, b_ocrd, local_sem.at[3])
    crd_copy.start()
    prods[0, NB] = jnp.zeros((BS, BS), jnp.float32)
    prods[1, NB] = jnp.zeros((BS, BS), jnp.float32)

    def ranked(pos, half):
        places, count = [], 0
        for e in range(2 * PIECE):
            inside = pos(1, e) // KB == half
            places.append(jnp.where(inside, count, -1))
            count = count + inside.astype(jnp.int32)
        return places

    owns = is_owner[0] | is_owner[1]
    load = pltpu.make_async_copy(a_hbm, a_full, local_sem.at[1])
    pl.when(owns)(load.start)

    pl.semaphore_wait(barrier, greeted)
    for d in range(1, YS):

        @pl.when(in_line & (y + d >= YS))
        def _():
            pl.semaphore_signal(line_ready, inc=1, device_id=y_peers[d - 1], device_id_type=MESH)


    @pl.when(last_plane)
    def _():
        pl.semaphore_signal(ready, inc=1, device_id=(below2, col), device_id_type=MESH)

    def remote(src, dst, send, recv, device):
        return pltpu.make_async_remote_copy(
            src_ref=src, dst_ref=dst, send_sem=send, recv_sem=recv,
            device_id=device, device_id_type=MESH,
        )

    crd_direct = remote(b_crd, b_gcrd, b_send.at[NCH], b_recv.at[NCH], (beside, col))
    crd_first = remote(b_crd, m_crd, b_send.at[NCH], m_recv.at[NCH], (beside, col))
    crd_second = remote(m_crd, b_gcrd, m_send.at[NCH], b_recv.at[NCH], (above2, col))
    direct, first, second = [], [], []
    for k in range(NCH):
        part = pl.ds(STARTS[k], CHUNKS[k])
        mid = b_mid.at[pl.ds(STARTS[k] % HALF, CHUNKS[k])]
        hops = (beside, above2) if k < BESIDE else (above2, beside)
        direct.append(
            remote(b_hbm.at[part], b_got.at[part], b_send.at[k], b_recv.at[k], (beside, col))
        )
        first.append(remote(b_hbm.at[part], mid, b_send.at[k], m_recv.at[k], (hops[0], col)))
        second.append(remote(mid, b_got.at[part], m_send.at[k], b_recv.at[k], (hops[1], col)))

    def stop(i):
        @pl.when(odds)
        def _():
            if i == 0:
                pl.when(first_plane)(lambda: pl.semaphore_wait(ready, 1))
                crd_first.wait_recv()
                crd_second.start()
            for k in STOPS_ODD[i]:
                first[k].wait_recv()
                second[k].start()

        @pl.when(evens)
        def _():
            for k in STOPS_EVEN[i]:
                first[k].wait_recv()
                second[k].start()

    def step_copies(s):
        blocks, crd = a_got.at[s], a_gcrd.at[s]
        send, recv = a_send.at[s], a_recv.at[s]
        theirs = [blocks.at[pl.ds(lax.rem(y + d, YS), 1)] for d in range(1, YS)]
        mine = blocks.at[pl.ds(y, 1)]
        one = [remote(theirs[d], theirs[d], send.at[S1 + d], recv.at[R1], y_peers[d]) for d in range(3)]
        one_crd = [remote(crd, crd, send.at[S1C + d], recv.at[RC], y_peers[d]) for d in range(3)]
        two = remote(mine, mine, send.at[S2], recv.at[R2], x_peer)
        two_crd = remote(crd, crd, send.at[S2C], recv.at[RC], x_peer)
        three = [remote(mine, mine, send.at[S3 + d], recv.at[R3 + d], y_peers[d]) for d in range(3)]
        four = remote(blocks, blocks, send.at[S4], recv.at[R4], core_peer)
        four_crd = remote(crd, crd, send.at[S4C], recv.at[RC], core_peer)
        return one, one_crd, two, two_crd, three, four, four_crd

    def not_owner(s, d):
        return (own_x[s] != x) | (own_y[s] != lax.rem(y + 1 + d, YS))

    @pl.when(evens)
    def _():
        first[0].start()
        crd_first.start()

    @pl.when(odds)
    def _():
        direct[0].start()
        crd_direct.start()

    pl.when(owns)(load.wait)
    waits = in_line & (y < YS - 1)
    pl.when(owns & waits)(lambda: pl.semaphore_wait(line_ready, YS - 1 - y))

    for s in range(STEPS):

        @pl.when(owners[s] == col)
        def _():
            crd = pltpu.make_async_copy(a_crd, a_gcrd.at[s], local_sem.at[2])
            crd.start()
            crd.wait()
            places = ranked(lambda i, e: a_pos[i, e], halves[s])
            for m in range(PIECE):
                which = 0
                for e in range(2 * PIECE):
                    which = which + jnp.where(places[e] == m, e, 0)
                a_got[s, m] = a_full[which]

    for s in range(STEPS):
        one, one_crd, two, two_crd, *_ = step_copies(s)

        @pl.when(is_owner[s])
        def _():
            for copy in [two_crd, two] + one_crd + one:
                copy.start()

    for s in range(STEPS):
        one, one_crd, two, two_crd, *_ = step_copies(s)

        @pl.when(holds[s] & jnp.logical_not(is_owner[s]))
        def _():
            one_crd[0].wait_recv()
            one[0].wait_recv()
            two_crd.start()
            two.start()

    @pl.when(odds)
    def _():
        for copy in direct[1:]:
            copy.start()

    @pl.when(evens)
    def _():
        for copy in first[1:BESIDE]:
            copy.start()
        pl.when(first_plane)(lambda: pl.semaphore_wait(ready, 1))
        for copy in first[BESIDE:]:
            copy.start()

    pl.when(waits & jnp.logical_not(owns))(lambda: pl.semaphore_wait(line_ready, YS - 1 - y))

    for s in range(STEPS):
        stop(s)
        one, one_crd, two, two_crd, three, four, four_crd = step_copies(s)

        @pl.when(own_core[s] == core)
        def _():
            @pl.when(own_x[s] != x)
            def _():
                two_crd.wait_recv()
                two.wait_recv()

            for d in range(3):
                pl.when(not_owner(s, d))(three[d].start)

            @pl.when(jnp.logical_not(is_owner[s]))
            def _():
                for copy in three:
                    copy.wait_recv()

            four_crd.start()
            four.start()

        @pl.when(own_core[s] != core)
        def _():
            four_crd.wait_recv()
            four.wait_recv()

        to_smem = pltpu.make_async_copy(a_gcrd.at[s], a_spos.at[s], local_sem.at[2])
        to_smem.start()
        to_smem.wait()

    stop(2)
    crd_direct.wait_recv()
    crd_copy.wait()

    picks = []
    for s in range(STEPS):
        places = ranked(lambda i, e: a_spos[s, i, e], halves[s])
        k_of, r_of = [], []
        for m in range(PIECE):
            k_m, r_m = 0, 0
            for e in range(2 * PIECE):
                k_m = k_m + jnp.where(places[e] == m, a_spos[s, 1, e], 0)
                r_m = r_m + jnp.where(places[e] == m, a_spos[s, 0, e], 0)
            k_of.append(k_m - halves[s] * KB)
            r_of.append(r_m)
        crd = b_ocrd if s == 0 else b_gcrd
        key = jnp.full((1, NB), PIECE * CB, jnp.int32)
        for m in range(PIECE):
            key = jnp.where(crd[0:1, :] == k_of[m], m * CB + crd[1:2, :], key)
        slot = lax.broadcasted_iota(jnp.int32, (PIECE * CB, NB), 0)
        entry = lax.broadcasted_iota(jnp.int32, (PIECE * CB, NB), 1)
        found = jnp.min(jnp.where(key == slot, entry, NB), axis=1, keepdims=True)
        tab_v[s, pl.ds(0, PIECE * CB), :] = jnp.broadcast_to(found, (PIECE * CB, BS))
        tab_v[s, pl.ds(PIECE * CB, 1), pl.ds(0, NB)] = jnp.minimum(key // CB, PIECE - 1)
        to_row = jnp.full((1, NB), RB, jnp.int32)
        for m in range(PIECE):
            to_row = jnp.where(key // CB == m, r_of[m], to_row)
        tab_v[s, pl.ds(PIECE * CB + 1, 1), pl.ds(0, NB)] = crd[1:2, :]
        tab_v[s, pl.ds(PIECE * CB + 2, 1), pl.ds(0, NB)] = to_row
        to_smem = pltpu.make_async_copy(tab_v.at[s], tab.at[s], local_sem.at[2])
        to_smem.start()
        to_smem.wait()
        picks.append(r_of)

    def multiply(s, blocks, first, count):
        def one_block(i, carry):
            n = first + i
            m = tab[s, PIECE * CB, n]
            prods[s, n] = jnp.dot(
                a_got[s, m], blocks[n],
                precision=lax.Precision.HIGHEST, preferred_element_type=jnp.float32,
            )
            return carry

        lax.fori_loop(0, count, one_block, 0, unroll=min(4, count) if count != 6 else 3)

    def gathered(s, c, r):
        terms = []
        for m in range(PIECE):
            n = jnp.where(picks[s][m] == r, tab[s, m * CB + c, 0], NB)
            terms.append(prods[s, n])
        return (terms[0] + terms[1]) + (terms[2] + terms[3])

    def spot(c, r):
        return (pl.ds(r * BS, BS), pl.ds(pl.multiple_of(c * BS, BS), BS))

    def early_term(c, carry):
        for r in range(RB):
            terms = []
            for m in range(PIECE):
                n = jnp.where(picks[1][m] == r, tab[1, m * CB + c, 0], NB)
                terms.append(prods[1, jnp.where(n < EARLY, n, NB)])
            total[spot(c, r)] = total[spot(c, r)] + ((terms[0] + terms[1]) + (terms[2] + terms[3]))
        return carry

    def late_term(c, carry):
        for r in range(RB):
            value = total[spot(c, r)]
            for n in range(EARLY, NB):
                key = tab[1, PIECE * CB + 1, n]
                hit = (key == c) & (tab[1, PIECE * CB + 2, n] == r)
                value = value + prods[1, jnp.where(hit, n, NB)]
            out[spot(c, r)] = value
        return carry

    own_copy.wait()
    multiply(0, b_own, 0, NB)
    stop(3)

    def first_term(c, carry):
        for r in range(RB):
            total[pl.ds(r * BS, BS), pl.ds(pl.multiple_of(c * BS, BS), BS)] = gathered(0, c, r)
        return carry

    lax.fori_loop(0, CB, first_term, 0, unroll=4)

    stop(4)
    for k in range(NCH - LATE):
        direct[k].wait_recv()
        multiply(1, b_got, STARTS[k], CHUNKS[k])

    lax.fori_loop(0, CB, early_term, 0, unroll=4)

    for k in range(NCH - LATE, NCH):
        direct[k].wait_recv()
        multiply(1, b_got, STARTS[k], CHUNKS[k])

    lax.fori_loop(0, CB, late_term, 0, unroll=4)

    for s in range(STEPS):
        one, one_crd, two, two_crd, three, four, four_crd = step_copies(s)

        @pl.when(is_owner[s])
        def _():
            for copy in one_crd + one:
                copy.wait_send()

        @pl.when(holds[s])
        def _():
            two_crd.wait_send()
            two.wait_send()

        @pl.when(own_core[s] == core)
        def _():
            for d in range(3):
                pl.when(not_owner(s, d))(three[d].wait_send)
            four_crd.wait_send()
            four.wait_send()

    crd_direct.wait_send()
    for copy in direct:
        copy.wait_send()

    @pl.when(evens)
    def _():
        for copy in second[BESIDE:]:
            copy.wait_send()

    @pl.when(odds)
    def _():
        for copy in [crd_second] + second[:BESIDE]:
            copy.wait_send()


def per_device(a_blocks, a_coords, b_blocks, b_coords):
    hbm = pl.BlockSpec(memory_space=pltpu.HBM)
    smem = pl.BlockSpec(memory_space=pltpu.SMEM)
    a_blk, a_pos = a_blocks[0, 0], a_coords[0, 0]
    b_blk, b_pos = b_blocks[0, 0], b_coords[0, 0]
    f32, i32 = jnp.float32, jnp.int32

    def kept(value):
        return pltpu.with_memory_space_constraint(value, pltpu.HBM)

    return pl.pallas_call(
        kernel,
        out_shape=jax.ShapeDtypeStruct((RB * BS, CB * BS), f32),
        in_specs=[hbm, hbm, smem, hbm, hbm],
        out_specs=pl.BlockSpec(memory_space=pltpu.VMEM),
        scratch_shapes=[
            pltpu.VMEM((2 * PIECE, BS, BS), f32),
            pltpu.VMEM((STEPS, PIECE, BS, BS), f32),
            pltpu.VMEM((STEPS, 2, 2 * PIECE), i32),
            pltpu.SMEM((STEPS, 2, 2 * PIECE), i32),
            pltpu.VMEM((NB, BS, BS), f32),
            pltpu.VMEM((NB, BS, BS), f32),
            pltpu.VMEM((HALF, BS, BS), f32),
            pltpu.VMEM((2, NB), i32),
            pltpu.VMEM((2, NB), i32),
            pltpu.VMEM((2, NB), i32),
            pltpu.VMEM((STEPS, PIECE * CB + 8, BS), i32),
            pltpu.SMEM((STEPS, PIECE * CB + 8, BS), i32),
            pltpu.VMEM((STEPS, NB + 1, BS, BS), f32),
            pltpu.VMEM((RB * BS, CB * BS), f32),
            pltpu.SemaphoreType.DMA((4,)),
            pltpu.SemaphoreType.DMA((NCH + 1,)),
            pltpu.SemaphoreType.DMA((NCH + 1,)),
            pltpu.SemaphoreType.DMA((NCH + 1,)),
            pltpu.SemaphoreType.DMA((NCH + 1,)),
            pltpu.SemaphoreType.DMA((STEPS, NS)),
            pltpu.SemaphoreType.DMA((STEPS, NR)),
            pltpu.SemaphoreType.REGULAR,
            pltpu.SemaphoreType.REGULAR,
        ],
        compiler_params=pltpu.CompilerParams(
            collective_id=0, has_side_effects=True, vmem_limit_bytes=48 << 20
        ),
    )(kept(a_blk), kept(a_pos), a_pos, kept(b_blk), kept(b_pos))


def solution(mesh):
    return jax.shard_map(
        per_device,
        mesh=mesh,
        in_specs=(
            P("row", "col", None, None, None),
            P("row", "col", None, None),
            P("row", "col", None, None, None),
            P("row", "col", None, None),
        ),
        out_specs=P("row", "col"),
        check_vma=False,
    )
```
